512 devices in a mesh: leaf: 128 (over z, x, core), vec: 4 (over y).
Axes of the slice: x: 4, y: 4, z: 16, core: 2. Of those that a mesh axis runs over, the one named last changes fastest.
Arguments:
- samples: bfloat16 [64, 524288], P('vec', 'leaf'), may hold values from -6 to 6
- coords: float32 [3, 524288], P(None, 'leaf'), may hold values from -4 to 4
- panel_area: float32 [524288], P('leaf'), may hold values from 0.05 to 0.5
- quad_weight: float32 [524288], P('leaf'), may hold values from 0.2 to 1
- leaf_basis: bfloat16 [2048, 64, 256], P('leaf'), may hold values from -0.375 to 0.375
- transfer: bfloat16 [1024, 2, 64, 64], P('leaf'), may hold values from -0.5 to 0.5
- coupling_fine: bfloat16 [2048, 16, 64, 64], P('leaf'), may hold values from -0.1875 to 0.1875
- coupling_coarse: bfloat16 [1024, 16, 64, 64], P('leaf'), may hold values from -0.1875 to 0.1875
- near_list: int32 [2048, 16], P('leaf'), may hold values from 0 to 2047, as said below
- send_fine: int32 [16384, 2], P('leaf'), may hold values from 0 to 15
- send_coarse: int32 [16384, 1], P('leaf'), may hold values from 0 to 7
- far_fine: int32 [2048, 16], P('leaf'), may hold values from 0 to 255, as said below
- far_coarse: int32 [1024, 16], P('leaf'), may hold values from 0 to 127, as said below
Outputs:
- sample_out: bfloat16 [64, 524288], P('vec', 'leaf')
- sample_gram: float32 [2048, 64, 64], P('leaf', 'vec')
The draws below stay inside these ranges and needn't reach their ends.
Inputs may be any that keep to these rules, and one draw needn't show every extreme that they name: `near_list`: row g names 16 different leaves, each at most 16 leaves from g. `send_fine`: row e * 128 + d names clusters of device e, counted on e from 0; every slot carries one. `send_coarse`: row e * 128 + d names clusters of device e, counted on e from 0; every slot carries one. `far_fine`: the rows of one device's 16 leaves name each of the values 0 to 255 exactly once. `far_coarse`: the rows of one device's parents name each of the values 0 to 127 exactly once.
All inputs are finite; a program needn't handle non-finite values.
Results may differ from the reference program's by a relative error of at most 0.0085.
Values may be sent and summed in bfloat16 or wider, within the bound.
No kernel may reach another device: no remote copies, remote signals or barrier semaphores. Data moves between devices by JAX's collectives and lax.ppermute only.
A program may use at most 64 MiB of HBM per device.

```python
import math
import jax
import jax.numpy as jnp
from jax import lax

LEAF = 256
K = 64
VECS = 64
NN = 16
HW = 16
NB = 16
LEAF_DEV = 16
LEAVES = 2048
POINTS = 524288
PARENTS = 1024
CAP0 = 2
CAP1 = 1
N_LEAF = 128


def draw_near_list(key, part):
    window_len = 2 * HW + 1
    offsets = jnp.arange(window_len, dtype=jnp.int32) - HW
    rank_bits = jax.random.randint(key, (LEAVES, window_len), 0, 1 << 20, dtype=jnp.int32)
    owner_leaf = jnp.arange(LEAVES, dtype=jnp.int32)[:, None]
    target = owner_leaf + offsets[None, :]
    inside = (target >= 0) & (target < LEAVES)
    scores = jnp.where(inside, rank_bits + (1 << 20), 0) * window_len + jnp.arange(window_len, dtype=jnp.int32)[None, :]
    top_scores, picked = lax.top_k(scores, NN)
    return jnp.take_along_axis(target, picked, axis=1).astype(jnp.int32)


def permuted_rows(key, per_device, width_nb):
    devices = LEAVES // LEAF_DEV
    device_keys = jax.random.split(key, devices)
    permuted = jax.vmap(lambda subkey: jax.random.permutation(subkey, per_device * width_nb))(device_keys)
    return permuted.reshape(devices * per_device, width_nb).astype(jnp.int32)


def draw_far_fine(key, part):
    return permuted_rows(jax.random.fold_in(key, 11), LEAF_DEV, NB)


def draw_far_coarse(key, part):
    return permuted_rows(jax.random.fold_in(key, 23), LEAF_DEV // 2, NB)


def touch_ends(values, key, least, largest):
    extent = values.shape
    place = [jax.random.randint(jax.random.fold_in(key, axis), (), 0, extent[axis]) for axis in range(len(extent))]
    values = values.at[tuple(place)].set(least)
    longest = extent.index(max(extent))
    place[longest] = (place[longest] + 1) % extent[longest]
    return values.at[tuple(place)].set(largest)


def block_levels(own_key, dims, cuts, least, largest):
    loudness, own = 1.0, jax.random.fold_in(own_key, 6)
    for dim, shards_of in cuts:
        steps = jnp.exp(jax.random.uniform(jax.random.fold_in(own, dim), (shards_of,), jnp.float32, least / len(cuts), largest / len(cuts)))
        loudness = loudness * jnp.repeat(steps, dims[dim] // shards_of).reshape([-1 if axis == dim else 1 for axis in range(len(dims))])
    return loudness


def centred(stream_key, shape, width, reach, pieces=(), held_as=jnp.bfloat16):
    result = width * jax.random.normal(stream_key, shape, jnp.float32)
    if pieces:
        result = result * block_levels(stream_key, shape, pieces, -0.22, 0.18)
    return jnp.clip(result, -reach, reach).astype(held_as)


def setup_inputs(seed: int = 0) -> dict:
    splits = jax.random.split(jax.random.key(seed), 14)
    return {
        "samples": centred(splits[0], (VECS, POINTS), 1.0, 6.0, ((0, 4), (1, 128))),
        "coords": centred(splits[1], (3, POINTS), 0.3, 4.0, ((1, 128),), jnp.float32),
        "panel_area": jnp.clip(jnp.exp(math.log(0.5) - 2.3025851 * jax.random.uniform(splits[2], (POINTS,), jnp.float32) ** block_levels(splits[2], (POINTS,), ((0, 128),), -0.2, 0.2)), 0.05, 0.5),
        "quad_weight": jnp.clip(0.2 + 0.8 * jax.random.uniform(splits[3], (POINTS,), jnp.float32) ** block_levels(splits[3], (POINTS,), ((0, 128),), -0.2, 0.2), 0.2, 1.0),
        "leaf_basis": centred(splits[4], (LEAVES, K, LEAF), LEAF ** -0.5, 0.375, ((0, 128),)),
        "transfer": centred(splits[5], (PARENTS, 2, K, K), (2 * K) ** -0.5, 0.5, ((0, 128),)),
        "coupling_fine": centred(splits[6], (LEAVES, NB, K, K), (NB * K) ** -0.5, 0.1875, ((0, 128),)),
        "coupling_coarse": centred(splits[7], (PARENTS, NB, K, K), (NB * K) ** -0.5, 0.1875, ((0, 128),)),
        "near_list": draw_near_list(jax.random.fold_in(splits[13], 71), 0),
        "send_fine": touch_ends(jax.random.randint(splits[9], (N_LEAF * N_LEAF, CAP0), 0, LEAF_DEV), jax.random.fold_in(splits[9], 1), 0, LEAF_DEV - 1).astype(jnp.int32),
        "send_coarse": touch_ends(jax.random.randint(splits[10], (N_LEAF * N_LEAF, CAP1), 0, LEAF_DEV // 2), jax.random.fold_in(splits[10], 1), 0, (LEAF_DEV // 2) - 1).astype(jnp.int32),
        "far_fine": draw_far_fine(jax.random.fold_in(splits[13], 71), 0),
        "far_coarse": draw_far_coarse(jax.random.fold_in(splits[13], 71), 0),
    }


four_pi = 4.0 * 3.141592653589793

def kernel_block(target, source):
    delta_x = target[0][:, None] - source[0][None, :]
    delta_y = target[1][:, None] - source[1][None, :]
    delta_z = target[2][:, None] - source[2][None, :]
    distance = delta_x * delta_x + delta_y * delta_y + delta_z * delta_z + source[3][None, :]
    return (source[4][None, :] / (four_pi * jnp.sqrt(distance))).astype(jnp.bfloat16)

def near_field(samples, geometry, near_list):
    leaves = near_list.shape[0]
    geo_all = geometry.reshape(5, leaves, LEAF)
    values = samples.reshape(samples.shape[0], leaves, LEAF)

    def leaf_group(indices):

        def one_leaf(index):
            chosen = near_list[index]
            src_geo = jnp.take(geo_all, chosen, axis=1)
            src_val = jnp.take(values, chosen, axis=1).astype(jnp.float32)
            target = jnp.take(geo_all[:3], index, axis=1)
            blocks = jax.vmap(kernel_block, (None, 1))(target, src_geo)
            return jnp.einsum('npq,vnq->vp', blocks.astype(jnp.float32), src_val)
        return jax.vmap(one_leaf)(indices)
    results = lax.map(leaf_group, jnp.arange(leaves, dtype=jnp.int32).reshape(-1, 8))
    return results.reshape(leaves, samples.shape[0], LEAF)

def partner_map(far_list, send_plan, per_device):
    slots = send_plan.shape[1]
    devices = far_list.shape[0] // per_device
    owner_dev = (jnp.arange(far_list.shape[0], dtype=jnp.int32) // per_device)[:, None]
    source = far_list // slots
    slot_index = far_list % slots
    local_index = send_plan[source * devices + owner_dev, slot_index]
    return (source * per_device + local_index).astype(jnp.int32)

def couple(tile_set, coef_table, partners, per_device):
    devices = partners.shape[0] // per_device
    width_nb = partners.shape[1]
    tile_set = tile_set.reshape(devices, per_device, width_nb, K, K)
    partners = partners.reshape(devices, per_device, width_nb)

    def one_device(operands):
        tiles, chosen = operands
        picked = coef_table[chosen].astype(jnp.float32)
        return jnp.einsum('ibkl,ibvl->ivk', tiles.astype(jnp.float32), picked)
    results = lax.map(one_device, (tile_set, partners))
    return results.reshape(devices * per_device, coef_table.shape[1], K)

def reference(samples, coords, panel_area, quad_weight, leaf_basis, transfer, coupling_fine, coupling_coarse, near_list, send_fine, send_coarse, far_fine, far_coarse):
    vectors = samples.shape[0]
    leaves = leaf_basis.shape[0]
    geometry = jnp.concatenate([coords, panel_area[None, :], quad_weight[None, :]], axis=0)
    near_part = near_field(samples, geometry, near_list)
    local_rows = samples.reshape(vectors, leaves, LEAF).astype(jnp.float32)
    fine_coef = jnp.einsum('ikp,vip->ivk', leaf_basis.astype(jnp.float32), local_rows).astype(jnp.bfloat16)
    coarse_coef = jnp.einsum('mskl,msvk->mvl', transfer.astype(jnp.float32), fine_coef.reshape(-1, 2, vectors, K).astype(jnp.float32)).astype(jnp.bfloat16)
    fine_partners = partner_map(far_fine, send_fine, LEAF_DEV)
    coarse_partners = partner_map(far_coarse, send_coarse, LEAF_DEV // 2)
    field_fine = couple(coupling_fine, fine_coef, fine_partners, LEAF_DEV)
    field_coarse = couple(coupling_coarse, coarse_coef, coarse_partners, LEAF_DEV // 2).astype(jnp.bfloat16)
    pushed = jnp.einsum('mskl,mvl->msvk', transfer.astype(jnp.float32), field_coarse.astype(jnp.float32))
    local_field = (field_fine + pushed.reshape(leaves, vectors, K)).astype(jnp.bfloat16)
    far_part = jnp.einsum('ikp,ivk->vip', leaf_basis.astype(jnp.float32), local_field.astype(jnp.float32))
    sample_out = (jnp.transpose(near_part, (1, 0, 2)) + far_part).reshape(vectors, leaves * LEAF).astype(jnp.bfloat16)
    shaped = sample_out.reshape(vectors, leaves, LEAF).astype(jnp.float32)
    sample_gram = jnp.einsum('aip,cip->iac', shaped, shaped) * (1.0 / LEAF)
    return (sample_out, sample_gram)
```

```python
import jax
import jax.numpy as jnp
from jax import lax
from jax.experimental import pallas as pl
from jax.experimental.pallas import tpu as pltpu
from jax.sharding import PartitionSpec as P

HW = 16
LANES = 128
FEATURES = 16
TERMS = 32
PAIRS = ((0, 0), (0, 1), (1, 0), (1, 1), (0, 2), (2, 0))

bf16 = jnp.bfloat16
f32 = jnp.float32
VM = pl.BlockSpec(memory_space=pltpu.VMEM)
SM = pl.BlockSpec(memory_space=pltpu.SMEM)
NT = (((1,), (1,)), ((), ()))
TN = (((0,), (0,)), ((), ()))


def params(mebibytes):
    return pltpu.CompilerParams(vmem_limit_bytes=mebibytes << 20)


def split3(x):
    hi = x.astype(bf16).astype(f32)
    rest = x - hi
    mid = rest.astype(bf16).astype(f32)
    return [hi, mid, rest - mid]


def term_rows():
    target, source = [], []
    for group in range(4):
        for first, second in PAIRS:
            target.append(3 * group + first)
            source.append((0, 6, 9, 12)[group] + second)
    for part in range(3):
        target.append(12)
        source.append(3 + part)
    return target, source


def selection(chosen, row, column):
    found = jnp.zeros(row.shape, f32)
    for place, index in enumerate(chosen):
        found = jnp.where((row == place) & (column == index), 1.0, found)
    return found.astype(bf16)


def source_kernel(samples_ref, coords_ref, area_ref, weight_ref, out_ref):
    vec_dev = samples_ref.shape[0]
    out_ref[0:vec_dev, :] = samples_ref[...]
    x, y, z = coords_ref[0:1, :], coords_ref[1:2, :], coords_ref[2:3, :]
    weight = weight_ref[...]
    scale = (16.0 * 3.141592653589793**2) / (weight * weight)
    shift = scale * (x * x + y * y + z * z + area_ref[...])
    rows = split3(scale) + split3(shift)
    for axis in (x, y, z):
        rows += split3(-2.0 * scale * axis)
    rows.append(jnp.zeros_like(scale))
    out_ref[vec_dev:, :] = jnp.concatenate(rows, axis=0).astype(bf16)


def source_rows(samples, coords, panel_area, quad_weight):
    vec_dev, points = samples.shape
    return pl.pallas_call(
        source_kernel,
        out_shape=jax.ShapeDtypeStruct((vec_dev + FEATURES, points), bf16),
        in_specs=[VM] * 4,
        out_specs=VM,
        compiler_params=params(6),
        name="source_rows",
    )(samples, coords, panel_area.reshape(1, -1), quad_weight.reshape(1, -1))


def coef_kernel(fine_ref, coarse_ref, samples_ref, basis_ref, transfer_ref, out_ref, table):
    leaf_dev, rank, pts = basis_ref.shape
    half = samples_ref.shape[0] // 2
    devices = fine_ref.shape[1]
    fine = []

    def keep(at, value):
        table[at] = jnp.concatenate([value[:half], value[half:]], axis=1).astype(bf16)

    for leaf in range(leaf_dev):
        value = lax.dot_general(
            samples_ref[:, leaf * pts : (leaf + 1) * pts],
            basis_ref[leaf],
            NT,
            preferred_element_type=f32,
        )
        keep(leaf, value)
        fine.append(value.astype(bf16))
    for parent in range(leaf_dev // 2):
        value = jnp.dot(fine[2 * parent], transfer_ref[parent, 0], preferred_element_type=f32)
        value += jnp.dot(fine[2 * parent + 1], transfer_ref[parent, 1], preferred_element_type=f32)
        keep(leaf_dev + parent, value)

    slots, parents = fine_ref.shape[0], coarse_ref.shape[0]
    width = slots + parents

    def fill(device, carry):
        for s in range(slots):
            out_ref[device * width + s] = table[fine_ref[s, device]]
        for s in range(parents):
            out_ref[device * width + slots + s] = table[leaf_dev + coarse_ref[s, device]]
        return carry

    lax.fori_loop(0, devices, fill, 0, unroll=8)


def send_rows(send_fine, send_coarse, samples, leaf_basis, transfer):
    leaf_dev, rank, _ = leaf_basis.shape
    half = samples.shape[0] // 2
    devices = send_fine.shape[0]
    width = send_fine.shape[1] + send_coarse.shape[1]
    return pl.pallas_call(
        coef_kernel,
        out_shape=jax.ShapeDtypeStruct((devices * width, half, 2 * rank), bf16),
        in_specs=[SM, SM] + [VM] * 3,
        out_specs=VM,
        scratch_shapes=[pltpu.VMEM((leaf_dev + leaf_dev // 2, half, 2 * rank), bf16)],
        compiler_params=params(8),
        name="send_rows",
    )(send_fine.T, send_coarse.T, samples, leaf_basis, transfer)


def near_kernel(first_ref, list_ref, coords_ref, own_ref, low_ref, high_ref, out_ref, feat, vals):
    vec_dev = out_ref.shape[0]
    leaf_dev, partners = list_ref.shape
    pts = feat.shape[2]
    target_rows, source_rows_ = term_rows()
    wide = selection(
        source_rows_,
        lax.broadcasted_iota(jnp.int32, (TERMS, FEATURES), 0),
        lax.broadcasted_iota(jnp.int32, (TERMS, FEATURES), 1),
    )
    tall = selection(
        target_rows,
        lax.broadcasted_iota(jnp.int32, (FEATURES, TERMS), 1),
        lax.broadcasted_iota(jnp.int32, (FEATURES, TERMS), 0),
    )
    for place, part in enumerate((low_ref, own_ref, high_ref)):
        for leaf in range(leaf_dev):
            cols = slice(leaf * pts, (leaf + 1) * pts)
            feat[place * leaf_dev + leaf] = jnp.dot(
                wide, part[vec_dev:, cols], preferred_element_type=f32
            ).astype(bf16)
            vals[place * leaf_dev + leaf] = part[0:vec_dev, cols]

    def one_leaf(leaf, carry):
        cols = pl.ds(pl.multiple_of(leaf * pts, pts), pts)
        x, y, z = coords_ref[0:1, cols], coords_ref[1:2, cols], coords_ref[2:3, cols]
        rows = split3(x * x + y * y + z * z) + split3(x) + split3(y) + split3(z)
        rows += [jnp.ones_like(x)] + [jnp.zeros_like(x)] * 3
        pieces = jnp.concatenate(rows, axis=0).astype(bf16)
        target = lax.dot_general(pieces, tall, TN, preferred_element_type=f32).astype(bf16)
        total = jnp.zeros((pts, vec_dev), f32)
        for n in range(partners):
            at = list_ref[leaf, n] - first_ref[0]
            dist = jnp.dot(target, feat[at], preferred_element_type=f32)
            block = lax.rsqrt(dist.astype(bf16))
            total += lax.dot_general(block, vals[at], NT, preferred_element_type=f32)
        out_ref[:, cols] = total.T
        return carry

    lax.fori_loop(0, leaf_dev, one_leaf, 0)


def near_field(first, near_list, coords, own, low, high, pts):
    vec_dev = own.shape[0] - FEATURES
    leaf_dev, partners = near_list.shape
    points = coords.shape[1]
    pairs = leaf_dev * partners * pts * pts
    return pl.pallas_call(
        near_kernel,
        out_shape=jax.ShapeDtypeStruct((vec_dev, points), f32),
        in_specs=[SM, SM] + [VM] * 4,
        out_specs=VM,
        scratch_shapes=[
            pltpu.VMEM((3 * leaf_dev, TERMS, pts), bf16),
            pltpu.VMEM((3 * leaf_dev, vec_dev, pts), bf16),
        ],
        compiler_params=params(8),
        cost_estimate=pl.CostEstimate(
            flops=2 * 512 * pairs, transcendentals=pairs, bytes_accessed=4 << 20
        ),
        name="near_field",
    )(first, near_list, coords, own, low, high)


def far_kernel(
    fine_list_ref,
    coarse_list_ref,
    got_ref,
    fine_ref,
    coarse_ref,
    transfer_ref,
    basis_ref,
    near_ref,
    out_ref,
    copies_ref,
):
    leaf_dev, partners = fine_list_ref.shape
    width = 3
    rank, pts = basis_ref.shape[1:]

    def field(tiles_ref, list_ref, at, place):
        total = None
        for b in range(partners):
            row = got_ref[place(list_ref[at, b])]
            rows = jnp.concatenate([row[:, :rank], row[:, rank:]], axis=0)
            part = lax.dot_general(rows, tiles_ref[at, b], NT, preferred_element_type=f32)
            total = part if total is None else total + part
        return total

    def one_parent(parent, carry):
        coarse = field(coarse_ref, coarse_list_ref, parent, lambda r: r * width + 2).astype(bf16)
        for child in range(2):
            leaf = 2 * parent + child
            local = field(fine_ref, fine_list_ref, leaf, lambda r: (r // 2) * width + r % 2)
            local += lax.dot_general(
                coarse, transfer_ref[parent, child], NT, preferred_element_type=f32
            )
            cols = pl.ds(pl.multiple_of(leaf * pts, pts), pts)
            far = jnp.dot(local.astype(bf16), basis_ref[leaf], preferred_element_type=f32)
            value = (near_ref[:, cols] + far).astype(bf16)
            out_ref[:, cols] = value
            for copy in range(copies_ref.shape[0]):
                copies_ref[copy, :, cols] = value
        return carry

    lax.fori_loop(0, leaf_dev // 2, one_parent, 0)


def far_field(
    far_fine, far_coarse, got, coupling_fine, coupling_coarse, transfer, basis, near, copies
):
    vec_dev, points = near.shape
    return pl.pallas_call(
        far_kernel,
        out_shape=(
            jax.ShapeDtypeStruct((vec_dev, points), bf16),
            jax.ShapeDtypeStruct((copies, vec_dev, points), bf16),
        ),
        in_specs=[SM, SM] + [VM] * 6,
        out_specs=(VM, VM),
        compiler_params=params(20),
        name="far_field",
    )(far_fine, far_coarse, got, coupling_fine, coupling_coarse, transfer, basis, near)


def gram_kernel(own_ref, all_ref, out_ref):
    leaf_dev = out_ref.shape[0]
    pts = own_ref.shape[1] // leaf_dev
    for leaf in range(leaf_dev):
        cols = slice(leaf * pts, (leaf + 1) * pts)
        out_ref[leaf] = lax.dot_general(
            own_ref[:, cols], all_ref[:, cols], NT, preferred_element_type=f32
        ) * (1.0 / pts)


def gram(own, rows, leaf_dev):
    return pl.pallas_call(
        gram_kernel,
        out_shape=jax.ShapeDtypeStruct((leaf_dev, own.shape[0], rows.shape[0]), f32),
        in_specs=[VM, VM],
        out_specs=VM,
        compiler_params=params(6),
        name="gram",
    )(own, rows)


def per_device(
    samples,
    coords,
    panel_area,
    quad_weight,
    leaf_basis,
    transfer,
    coupling_fine,
    coupling_coarse,
    near_list,
    send_fine,
    send_coarse,
    far_fine,
    far_coarse,
):
    vec_dev, points = samples.shape
    leaf_dev, rank, pts = leaf_basis.shape
    devices = lax.axis_size("leaf")
    groups = lax.axis_size("vec")
    device = lax.axis_index("leaf")

    own = source_rows(samples, coords, panel_area, quad_weight)
    forward = [(i, i + 1) for i in range(devices - 1)]
    backward = [(i + 1, i) for i in range(devices - 1)]
    low = lax.ppermute(own, "leaf", forward)
    high = lax.ppermute(own, "leaf", backward)

    sent = send_rows(send_fine, send_coarse, samples, leaf_basis, transfer)
    half = sent.shape[1]
    got = lax.all_to_all(
        sent.reshape(devices, -1, LANES), "leaf", split_axis=0, concat_axis=0, tiled=True
    ).reshape(-1, half, LANES)

    first = (device * leaf_dev - HW).astype(jnp.int32).reshape(1)
    near = near_field(first, near_list, coords, own, low, high, pts)
    sample_out, copies = far_field(
        far_fine, far_coarse, got, coupling_fine, coupling_coarse, transfer, leaf_basis, near, groups
    )
    rows = lax.all_to_all(copies, "vec", split_axis=0, concat_axis=0, tiled=True)
    sample_gram = gram(sample_out, rows.reshape(groups * vec_dev, points), leaf_dev)
    return (sample_out, sample_gram)


def solution(mesh):
    return jax.shard_map(
        per_device,
        mesh=mesh,
        in_specs=(
            P("vec", "leaf"),
            P(None, "leaf"),
            P("leaf"),
            P("leaf"),
            P("leaf", None, None),
            P("leaf", None, None, None),
            P("leaf", None, None, None),
            P("leaf", None, None, None),
            P("leaf", None),
            P("leaf", None),
            P("leaf", None),
            P("leaf", None),
            P("leaf", None),
        ),
        out_specs=(P("vec", "leaf"), P("leaf", "vec", None)),
        check_vma=False,
    )
```

```python
import jax
import jax.numpy as jnp
from jax import lax
from jax.experimental import pallas as pl
from jax.experimental.pallas import tpu as pltpu
from jax.sharding import PartitionSpec as P

HW = 16
LANES = 128
FEATURES = 16
TERMS = 32
PAIRS = ((0, 0), (0, 1), (1, 0), (1, 1), (0, 2), (2, 0))

bf16 = jnp.bfloat16
f32 = jnp.float32
VM = pl.BlockSpec(memory_space=pltpu.VMEM)
SM = pl.BlockSpec(memory_space=pltpu.SMEM)
HB = pl.BlockSpec(memory_space=pltpu.HBM)
NT = (((1,), (1,)), ((), ()))
TN = (((0,), (0,)), ((), ()))


def params(mebibytes):
    return pltpu.CompilerParams(vmem_limit_bytes=mebibytes << 20)


def start_all(pairs, sems):
    copies = [pltpu.make_async_copy(a, b, sems.at[n]) for n, (a, b) in enumerate(pairs)]
    for copy in copies:
        copy.start()
    return copies


def wait_all(copies):
    for copy in copies:
        copy.wait()


def split3(x):
    hi = x.astype(bf16).astype(f32)
    rest = x - hi
    mid = rest.astype(bf16).astype(f32)
    return [hi, mid, rest - mid]


def term_rows():
    target, source = [], []
    for group in range(4):
        for first, second in PAIRS:
            target.append(3 * group + first)
            source.append((0, 6, 9, 12)[group] + second)
    for part in range(3):
        target.append(12)
        source.append(3 + part)
    return target, source


def selection(chosen, row, column):
    found = jnp.zeros(row.shape, f32)
    for place, index in enumerate(chosen):
        found = jnp.where((row == place) & (column == index), 1.0, found)
    return found.astype(bf16)


def source_kernel(samples_hbm, coords_hbm, area_hbm, weight_hbm, out_hbm, rows_v, coords_ref, area_ref, weight_ref, sems):
    vec_dev = samples_hbm.shape[0]
    copies = start_all(
        [
            (coords_hbm, coords_ref),
            (area_hbm, area_ref),
            (weight_hbm, weight_ref),
            (samples_hbm, rows_v.at[0:vec_dev]),
        ],
        sems,
    )
    wait_all(copies[:3])
    x, y, z = coords_ref[0:1, :], coords_ref[1:2, :], coords_ref[2:3, :]
    weight = weight_ref[...]
    scale = (16.0 * 3.141592653589793**2) / (weight * weight)
    shift = scale * (x * x + y * y + z * z + area_ref[...])
    rows = split3(scale) + split3(shift)
    for axis in (x, y, z):
        rows += split3(-2.0 * scale * axis)
    rows.append(jnp.zeros_like(scale))
    rows_v[vec_dev:, :] = jnp.concatenate(rows, axis=0).astype(bf16)
    copies[3].wait()
    wait_all(start_all([(rows_v, out_hbm)], sems))


def source_rows(samples, coords, panel_area, quad_weight):
    vec_dev, points = samples.shape
    shape = (vec_dev + FEATURES, points)
    return pl.pallas_call(
        source_kernel,
        out_shape=jax.ShapeDtypeStruct(shape, bf16),
        in_specs=[HB] * 4,
        out_specs=HB,
        scratch_shapes=[
            pltpu.VMEM(shape, bf16),
            pltpu.VMEM(coords.shape, f32),
            pltpu.VMEM((1, points), f32),
            pltpu.VMEM((1, points), f32),
            pltpu.SemaphoreType.DMA((4,)),
        ],
        compiler_params=params(60),
        name="source_rows",
    )(samples, coords, panel_area.reshape(1, -1), quad_weight.reshape(1, -1))


def coef_kernel(
    fine_hbm,
    coarse_hbm,
    own_hbm,
    basis_hbm,
    transfer_hbm,
    out_ref,
    table,
    fine_ref,
    coarse_ref,
    samples_ref,
    basis_ref,
    transfer_ref,
    sems,
):
    leaf_dev, rank, pts = basis_ref.shape
    half = samples_ref.shape[0] // 2
    devices = fine_ref.shape[1]
    copies = start_all(
        [
            (own_hbm.at[0 : 2 * half], samples_ref),
            (basis_hbm, basis_ref),
            (transfer_hbm, transfer_ref),
            (fine_hbm, fine_ref),
            (coarse_hbm, coarse_ref),
        ],
        sems,
    )
    fine = []

    def keep(at, value):
        table[at] = jnp.concatenate([value[:half], value[half:]], axis=1).astype(bf16)

    wait_all(copies[:2])
    for leaf in range(leaf_dev):
        value = lax.dot_general(
            samples_ref[:, leaf * pts : (leaf + 1) * pts],
            basis_ref[leaf],
            NT,
            preferred_element_type=f32,
        )
        keep(leaf, value)
        fine.append(value.astype(bf16))
    copies[2].wait()
    for parent in range(leaf_dev // 2):
        value = jnp.dot(fine[2 * parent], transfer_ref[parent, 0], preferred_element_type=f32)
        value += jnp.dot(fine[2 * parent + 1], transfer_ref[parent, 1], preferred_element_type=f32)
        keep(leaf_dev + parent, value)

    wait_all(copies[3:])
    slots, parents = fine_ref.shape[0], coarse_ref.shape[0]
    width = slots + parents

    def fill(device, carry):
        for s in range(slots):
            out_ref[device * width + s] = table[fine_ref[s, device]]
        for s in range(parents):
            out_ref[device * width + slots + s] = table[leaf_dev + coarse_ref[s, device]]
        return carry

    lax.fori_loop(0, devices, fill, 0, unroll=8)


def send_rows(send_fine, send_coarse, own, leaf_basis, transfer):
    leaf_dev, rank, pts = leaf_basis.shape
    vec_dev = own.shape[0] - FEATURES
    half = vec_dev // 2
    devices = send_fine.shape[0]
    width = send_fine.shape[1] + send_coarse.shape[1]
    return pl.pallas_call(
        coef_kernel,
        out_shape=jax.ShapeDtypeStruct((devices * width, half, 2 * rank), bf16),
        in_specs=[HB] * 5,
        out_specs=VM,
        scratch_shapes=[
            pltpu.VMEM((leaf_dev + leaf_dev // 2, half, 2 * rank), bf16),
            pltpu.SMEM(send_fine.shape[::-1], jnp.int32),
            pltpu.SMEM(send_coarse.shape[::-1], jnp.int32),
            pltpu.VMEM((vec_dev, own.shape[1]), bf16),
            pltpu.VMEM(leaf_basis.shape, bf16),
            pltpu.VMEM(transfer.shape, bf16),
            pltpu.SemaphoreType.DMA((5,)),
        ],
        compiler_params=params(60),
        name="send_rows",
    )(send_fine.T, send_coarse.T, own, leaf_basis, transfer)


def near_kernel(
    first_ref,
    list_hbm,
    coords_hbm,
    own_hbm,
    low_hbm,
    high_hbm,
    out_hbm,
    feat,
    vals,
    list_ref,
    coords_ref,
    own_ref,
    low_ref,
    high_ref,
    out_ref,
    sems,
):
    vec_dev = out_ref.shape[0]
    leaf_dev, partners = list_ref.shape
    pts = feat.shape[2]
    copies = start_all(
        [
            (own_hbm, own_ref),
            (low_hbm, low_ref),
            (high_hbm, high_ref),
            (list_hbm, list_ref),
            (coords_hbm, coords_ref),
        ],
        sems,
    )
    target_rows, source_rows_ = term_rows()
    wide = selection(
        source_rows_,
        lax.broadcasted_iota(jnp.int32, (TERMS, FEATURES), 0),
        lax.broadcasted_iota(jnp.int32, (TERMS, FEATURES), 1),
    )
    tall = selection(
        target_rows,
        lax.broadcasted_iota(jnp.int32, (FEATURES, TERMS), 1),
        lax.broadcasted_iota(jnp.int32, (FEATURES, TERMS), 0),
    )
    wait_all(copies)
    for place, part in enumerate((low_ref, own_ref, high_ref)):
        for leaf in range(leaf_dev):
            cols = slice(leaf * pts, (leaf + 1) * pts)
            feat[place * leaf_dev + leaf] = jnp.dot(
                wide, part[vec_dev:, cols], preferred_element_type=f32
            ).astype(bf16)
            vals[place * leaf_dev + leaf] = part[0:vec_dev, cols]

    def one_leaf(leaf, carry):
        cols = pl.ds(pl.multiple_of(leaf * pts, pts), pts)
        x, y, z = coords_ref[0:1, cols], coords_ref[1:2, cols], coords_ref[2:3, cols]
        rows = split3(x * x + y * y + z * z) + split3(x) + split3(y) + split3(z)
        rows += [jnp.ones_like(x)] + [jnp.zeros_like(x)] * 3
        pieces = jnp.concatenate(rows, axis=0).astype(bf16)
        target = lax.dot_general(pieces, tall, TN, preferred_element_type=f32).astype(bf16)
        total = jnp.zeros((pts, vec_dev), f32)
        for n in range(partners):
            at = list_ref[leaf, n] - first_ref[0]
            dist = jnp.dot(target, feat[at], preferred_element_type=f32)
            block = lax.rsqrt(dist.astype(bf16))
            total += lax.dot_general(block, vals[at], NT, preferred_element_type=f32)
        out_ref[:, cols] = total.T
        return carry

    lax.fori_loop(0, leaf_dev, one_leaf, 0)
    wait_all(start_all([(out_ref, out_hbm)], sems))


def near_field(first, near_list, coords, own, low, high, pts):
    vec_dev = own.shape[0] - FEATURES
    leaf_dev, partners = near_list.shape
    points = coords.shape[1]
    pairs = leaf_dev * partners * pts * pts
    return pl.pallas_call(
        near_kernel,
        out_shape=jax.ShapeDtypeStruct((vec_dev, points), f32),
        in_specs=[SM] + [HB] * 5,
        out_specs=HB,
        scratch_shapes=[
            pltpu.VMEM((3 * leaf_dev, TERMS, pts), bf16),
            pltpu.VMEM((3 * leaf_dev, vec_dev, pts), bf16),
            pltpu.SMEM(near_list.shape, jnp.int32),
            pltpu.VMEM(coords.shape, f32),
            pltpu.VMEM(own.shape, bf16),
            pltpu.VMEM(own.shape, bf16),
            pltpu.VMEM(own.shape, bf16),
            pltpu.VMEM((vec_dev, points), f32),
            pltpu.SemaphoreType.DMA((5,)),
        ],
        compiler_params=params(60),
        cost_estimate=pl.CostEstimate(
            flops=2 * 512 * pairs, transcendentals=pairs, bytes_accessed=4 << 20
        ),
        name="near_field",
    )(first, near_list, coords, own, low, high)


def far_kernel(
    fine_list_hbm,
    coarse_list_hbm,
    got_hbm,
    fine_hbm,
    coarse_hbm,
    transfer_hbm,
    basis_hbm,
    near_hbm,
    out_ref,
    copies_ref,
    fine_list_ref,
    coarse_list_ref,
    got_ref,
    fine_ref,
    coarse_ref,
    transfer_ref,
    basis_ref,
    near_ref,
    sems,
    fine_sems,
    coarse_sems,
):
    leaf_dev, partners = fine_list_ref.shape
    width = 3
    rank, pts = basis_ref.shape[1:]
    half = got_ref.shape[1]
    copies = start_all(
        [
            (coarse_list_hbm, coarse_list_ref),
            (fine_list_hbm, fine_list_ref),
            (got_hbm, got_ref),
            (transfer_hbm, transfer_ref),
            (basis_hbm, basis_ref),
            (near_hbm, near_ref),
        ],
        sems,
    )

    def blocks(parent):
        two = pl.ds(2 * parent, 2)
        return (
            pltpu.make_async_copy(
                coarse_hbm.at[parent], coarse_ref.at[parent], coarse_sems.at[parent]
            ),
            pltpu.make_async_copy(fine_hbm.at[two], fine_ref.at[two], fine_sems.at[parent]),
        )

    for parent in range(leaf_dev // 2):
        for copy in blocks(parent):
            copy.start()
    wait_all(copies)
    left = lax.broadcasted_iota(jnp.int32, (half, 2 * rank), 1) < rank

    def joined(first, second):
        first, second = first.astype(f32), second.astype(f32)
        return jnp.concatenate(
            [
                jnp.where(left, first, pltpu.roll(second, rank, 1)),
                jnp.where(left, pltpu.roll(first, rank, 1), second),
            ],
            axis=0,
        ).astype(bf16)

    def field(tiles_ref, list_ref, at, place):
        total = None
        for b in range(0, partners, 4):
            rows = [got_ref[place(list_ref[at, b + n])] for n in range(4)]
            rows = jnp.concatenate([joined(*rows[:2]), joined(*rows[2:])], axis=1)
            tiles = jnp.concatenate([tiles_ref[at, b + n] for n in range(4)], axis=1)
            part = lax.dot_general(rows, tiles, NT, preferred_element_type=f32)
            total = part if total is None else total + part
        return total

    def one_parent(parent, carry):
        for copy in blocks(parent):
            copy.wait()
        coarse = field(coarse_ref, coarse_list_ref, parent, lambda r: r * width + 2).astype(bf16)
        for child in range(2):
            leaf = 2 * parent + child
            local = field(fine_ref, fine_list_ref, leaf, lambda r: (r >> 1) * width + (r & 1))
            local += lax.dot_general(
                coarse, transfer_ref[parent, child], NT, preferred_element_type=f32
            )
            cols = pl.ds(pl.multiple_of(leaf * pts, pts), pts)
            far = jnp.dot(local.astype(bf16), basis_ref[leaf], preferred_element_type=f32)
            value = (near_ref[:, cols] + far).astype(bf16)
            out_ref[:, cols] = value
            for copy in range(copies_ref.shape[0]):
                copies_ref[copy, :, cols] = value
        return carry

    lax.fori_loop(0, leaf_dev // 2, one_parent, 0)


def far_field(
    far_fine, far_coarse, got, coupling_fine, coupling_coarse, transfer, basis, near, copies
):
    vec_dev, points = near.shape
    held = (got, coupling_fine, coupling_coarse, transfer, basis, near)
    parents = coupling_coarse.shape[0]
    return pl.pallas_call(
        far_kernel,
        out_shape=(
            jax.ShapeDtypeStruct((vec_dev, points), bf16),
            jax.ShapeDtypeStruct((copies, vec_dev, points), bf16),
        ),
        in_specs=[HB] * 8,
        out_specs=(VM, VM),
        scratch_shapes=[
            pltpu.SMEM(far_fine.shape, jnp.int32),
            pltpu.SMEM(far_coarse.shape, jnp.int32),
            *[pltpu.VMEM(a.shape, a.dtype) for a in held],
            pltpu.SemaphoreType.DMA((6,)),
            pltpu.SemaphoreType.DMA((parents,)),
            pltpu.SemaphoreType.DMA((parents,)),
        ],
        compiler_params=params(60),
        name="far_field",
    )(far_fine, far_coarse, *held)


def gram_kernel(me_ref, all_ref, out_ref):
    leaf_dev, vec_dev = out_ref.shape[:2]
    pts = all_ref.shape[1] // leaf_dev
    mine = pl.ds(pl.multiple_of(me_ref[0] * vec_dev, vec_dev), vec_dev)
    for leaf in range(leaf_dev):
        cols = slice(leaf * pts, (leaf + 1) * pts)
        out_ref[leaf] = lax.dot_general(
            all_ref[mine, cols], all_ref[:, cols], NT, preferred_element_type=f32
        ) * (1.0 / pts)


def gram(me, rows, vec_dev, leaf_dev):
    return pl.pallas_call(
        gram_kernel,
        out_shape=jax.ShapeDtypeStruct((leaf_dev, vec_dev, rows.shape[0]), f32),
        in_specs=[SM, VM],
        out_specs=VM,
        compiler_params=params(6),
        name="gram",
    )(me, rows)


def per_device(
    samples,
    coords,
    panel_area,
    quad_weight,
    leaf_basis,
    transfer,
    coupling_fine,
    coupling_coarse,
    near_list,
    send_fine,
    send_coarse,
    far_fine,
    far_coarse,
):
    vec_dev, points = samples.shape
    leaf_dev, rank, pts = leaf_basis.shape
    devices = lax.axis_size("leaf")
    groups = lax.axis_size("vec")
    device = lax.axis_index("leaf")

    own = source_rows(samples, coords, panel_area, quad_weight)
    forward = [(i, i + 1) for i in range(devices - 1)]
    backward = [(i + 1, i) for i in range(devices - 1)]
    low = lax.ppermute(own, "leaf", forward)
    high = lax.ppermute(own, "leaf", backward)

    sent = send_rows(send_fine, send_coarse, own, leaf_basis, transfer)
    half = sent.shape[1]
    sent, low, high = lax.optimization_barrier((sent, low, high))
    got = lax.all_to_all(
        sent.reshape(devices, -1, LANES), "leaf", split_axis=0, concat_axis=0, tiled=True
    ).reshape(-1, half, LANES)

    first = (device * leaf_dev - HW).astype(jnp.int32).reshape(1)
    near = near_field(first, near_list, coords, own, low, high, pts)
    sample_out, copies = far_field(
        far_fine, far_coarse, got, coupling_fine, coupling_coarse, transfer, leaf_basis, near, groups
    )
    rows = lax.all_to_all(copies, "vec", split_axis=0, concat_axis=0, tiled=True)
    me = lax.axis_index("vec").astype(jnp.int32).reshape(1)
    sample_gram = gram(me, rows.reshape(groups * vec_dev, points), vec_dev, leaf_dev)
    return (sample_out, sample_gram)


def solution(mesh):
    return jax.shard_map(
        per_device,
        mesh=mesh,
        in_specs=(
            P("vec", "leaf"),
            P(None, "leaf"),
            P("leaf"),
            P("leaf"),
            P("leaf", None, None),
            P("leaf", None, None, None),
            P("leaf", None, None, None),
            P("leaf", None, None, None),
            P("leaf", None),
            P("leaf", None),
            P("leaf", None),
            P("leaf", None),
            P("leaf", None),
        ),
        out_specs=(P("vec", "leaf"), P("leaf", "vec", None)),
        check_vma=False,
    )
```

```python
import jax
import jax.numpy as jnp
from jax import lax
from jax.experimental import pallas as pl
from jax.experimental.pallas import tpu as pltpu
from jax.sharding import PartitionSpec as P

HW = 16
LANES = 128
FEATURES = 16
TERMS = 32
PAIRS = ((0, 0), (0, 1), (1, 0), (1, 1), (0, 2), (2, 0))

bf16 = jnp.bfloat16
f32 = jnp.float32
VM = pl.BlockSpec(memory_space=pltpu.VMEM)
SM = pl.BlockSpec(memory_space=pltpu.SMEM)
HB = pl.BlockSpec(memory_space=pltpu.HBM)
NT = (((1,), (1,)), ((), ()))
TN = (((0,), (0,)), ((), ()))


def params(mebibytes):
    return pltpu.CompilerParams(vmem_limit_bytes=mebibytes << 20)


def start_all(pairs, sems):
    copies = [pltpu.make_async_copy(a, b, sems.at[n]) for n, (a, b) in enumerate(pairs)]
    for copy in copies:
        copy.start()
    return copies


def wait_all(copies):
    for copy in copies:
        copy.wait()


def split3(x):
    hi = x.astype(bf16).astype(f32)
    rest = x - hi
    mid = rest.astype(bf16).astype(f32)
    return [hi, mid, rest - mid]


def term_rows():
    target, source = [], []
    for group in range(4):
        for first, second in PAIRS:
            target.append(3 * group + first)
            source.append((0, 6, 9, 12)[group] + second)
    for part in range(3):
        target.append(12)
        source.append(3 + part)
    return target, source


def selection(chosen, row, column):
    found = jnp.zeros(row.shape, f32)
    for place, index in enumerate(chosen):
        found = jnp.where((row == place) & (column == index), 1.0, found)
    return found.astype(bf16)


def source_kernel(samples_hbm, coords_hbm, area_hbm, weight_hbm, out_hbm, rows_v, coords_ref, area_ref, weight_ref, sems):
    vec_dev = samples_hbm.shape[0]
    copies = start_all(
        [
            (coords_hbm, coords_ref),
            (area_hbm, area_ref),
            (weight_hbm, weight_ref),
            (samples_hbm, rows_v.at[0:vec_dev]),
        ],
        sems,
    )
    wait_all(copies[:3])
    x, y, z = coords_ref[0:1, :], coords_ref[1:2, :], coords_ref[2:3, :]
    weight = weight_ref[...]
    scale = (16.0 * 3.141592653589793**2) / (weight * weight)
    shift = scale * (x * x + y * y + z * z + area_ref[...])
    rows = split3(scale) + split3(shift)
    for axis in (x, y, z):
        rows += split3(-2.0 * scale * axis)
    rows.append(jnp.zeros_like(scale))
    rows_v[vec_dev:, :] = jnp.concatenate(rows, axis=0).astype(bf16)
    copies[3].wait()
    wait_all(start_all([(rows_v, out_hbm)], sems))


def source_rows(samples, coords, panel_area, quad_weight):
    vec_dev, points = samples.shape
    shape = (vec_dev + FEATURES, points)
    return pl.pallas_call(
        source_kernel,
        out_shape=jax.ShapeDtypeStruct(shape, bf16),
        in_specs=[HB] * 4,
        out_specs=HB,
        scratch_shapes=[
            pltpu.VMEM(shape, bf16),
            pltpu.VMEM(coords.shape, f32),
            pltpu.VMEM((1, points), f32),
            pltpu.VMEM((1, points), f32),
            pltpu.SemaphoreType.DMA((4,)),
        ],
        compiler_params=params(60),
        name="source_rows",
    )(samples, coords, panel_area.reshape(1, -1), quad_weight.reshape(1, -1))


def coef_kernel(
    fine_hbm,
    coarse_hbm,
    own_hbm,
    basis_hbm,
    transfer_hbm,
    out_ref,
    table,
    fine_ref,
    coarse_ref,
    samples_ref,
    basis_ref,
    transfer_ref,
    sems,
):
    leaf_dev, rank, pts = basis_ref.shape
    half = samples_ref.shape[0] // 2
    devices = fine_ref.shape[1]
    copies = start_all(
        [
            (own_hbm.at[0 : 2 * half], samples_ref),
            (basis_hbm, basis_ref),
            (transfer_hbm, transfer_ref),
            (fine_hbm, fine_ref),
            (coarse_hbm, coarse_ref),
        ],
        sems,
    )
    fine = []

    def keep(at, value):
        table[at] = jnp.concatenate([value[:half], value[half:]], axis=1).astype(bf16)

    wait_all(copies[:2])
    for leaf in range(leaf_dev):
        value = lax.dot_general(
            samples_ref[:, leaf * pts : (leaf + 1) * pts],
            basis_ref[leaf],
            NT,
            preferred_element_type=f32,
        )
        keep(leaf, value)
        fine.append(value.astype(bf16))
    copies[2].wait()
    for parent in range(leaf_dev // 2):
        value = jnp.dot(fine[2 * parent], transfer_ref[parent, 0], preferred_element_type=f32)
        value += jnp.dot(fine[2 * parent + 1], transfer_ref[parent, 1], preferred_element_type=f32)
        keep(leaf_dev + parent, value)

    wait_all(copies[3:])
    slots, parents = fine_ref.shape[0], coarse_ref.shape[0]
    width = slots + parents

    def fill(device, carry):
        for s in range(slots):
            out_ref[device * width + s] = table[fine_ref[s, device]]
        for s in range(parents):
            out_ref[device * width + slots + s] = table[leaf_dev + coarse_ref[s, device]]
        return carry

    lax.fori_loop(0, devices, fill, 0, unroll=8)


def send_rows(send_fine, send_coarse, own, leaf_basis, transfer):
    leaf_dev, rank, pts = leaf_basis.shape
    vec_dev = own.shape[0] - FEATURES
    half = vec_dev // 2
    devices = send_fine.shape[0]
    width = send_fine.shape[1] + send_coarse.shape[1]
    return pl.pallas_call(
        coef_kernel,
        out_shape=jax.ShapeDtypeStruct((devices * width, half, 2 * rank), bf16),
        in_specs=[HB] * 5,
        out_specs=VM,
        scratch_shapes=[
            pltpu.VMEM((leaf_dev + leaf_dev // 2, half, 2 * rank), bf16),
            pltpu.SMEM(send_fine.shape[::-1], jnp.int32),
            pltpu.SMEM(send_coarse.shape[::-1], jnp.int32),
            pltpu.VMEM((vec_dev, own.shape[1]), bf16),
            pltpu.VMEM(leaf_basis.shape, bf16),
            pltpu.VMEM(transfer.shape, bf16),
            pltpu.SemaphoreType.DMA((5,)),
        ],
        compiler_params=params(60),
        name="send_rows",
    )(send_fine.T, send_coarse.T, own, leaf_basis, transfer)


def near_kernel(
    first_ref,
    list_hbm,
    coords_hbm,
    own_hbm,
    low_hbm,
    high_hbm,
    out_hbm,
    feat,
    vals,
    list_ref,
    coords_ref,
    own_ref,
    low_ref,
    high_ref,
    out_ref,
    sems,
):
    vec_dev = out_ref.shape[0]
    leaf_dev, partners = list_ref.shape
    pts = feat.shape[2]
    copies = start_all(
        [
            (own_hbm, own_ref),
            (low_hbm, low_ref),
            (high_hbm, high_ref),
            (list_hbm, list_ref),
            (coords_hbm, coords_ref),
        ],
        sems,
    )
    target_rows, source_rows_ = term_rows()
    wide = selection(
        source_rows_,
        lax.broadcasted_iota(jnp.int32, (TERMS, FEATURES), 0),
        lax.broadcasted_iota(jnp.int32, (TERMS, FEATURES), 1),
    )
    tall = selection(
        target_rows,
        lax.broadcasted_iota(jnp.int32, (FEATURES, TERMS), 1),
        lax.broadcasted_iota(jnp.int32, (FEATURES, TERMS), 0),
    )
    wait_all(copies)
    for place, part in enumerate((low_ref, own_ref, high_ref)):
        for leaf in range(leaf_dev):
            cols = slice(leaf * pts, (leaf + 1) * pts)
            feat[place * leaf_dev + leaf] = jnp.dot(
                wide, part[vec_dev:, cols], preferred_element_type=f32
            ).astype(bf16)
            vals[place * leaf_dev + leaf] = part[0:vec_dev, cols]

    def one_leaf(leaf, carry):
        cols = pl.ds(pl.multiple_of(leaf * pts, pts), pts)
        x, y, z = coords_ref[0:1, cols], coords_ref[1:2, cols], coords_ref[2:3, cols]
        rows = split3(x * x + y * y + z * z) + split3(x) + split3(y) + split3(z)
        rows += [jnp.ones_like(x)] + [jnp.zeros_like(x)] * 3
        pieces = jnp.concatenate(rows, axis=0).astype(bf16)
        target = lax.dot_general(pieces, tall, TN, preferred_element_type=f32).astype(bf16)
        total = jnp.zeros((pts, vec_dev), f32)
        for n in range(partners):
            at = list_ref[leaf, n] - first_ref[0]
            dist = jnp.dot(target, feat[at], preferred_element_type=f32)
            block = lax.rsqrt(dist.astype(bf16))
            total += lax.dot_general(block, vals[at], NT, preferred_element_type=f32)
        out_ref[:, cols] = total.T
        return carry

    lax.fori_loop(0, leaf_dev, one_leaf, 0)
    wait_all(start_all([(out_ref, out_hbm)], sems))


def near_field(first, near_list, coords, own, low, high, pts):
    vec_dev = own.shape[0] - FEATURES
    leaf_dev, partners = near_list.shape
    points = coords.shape[1]
    pairs = leaf_dev * partners * pts * pts
    return pl.pallas_call(
        near_kernel,
        out_shape=jax.ShapeDtypeStruct((vec_dev, points), f32),
        in_specs=[SM] + [HB] * 5,
        out_specs=HB,
        scratch_shapes=[
            pltpu.VMEM((3 * leaf_dev, TERMS, pts), bf16),
            pltpu.VMEM((3 * leaf_dev, vec_dev, pts), bf16),
            pltpu.SMEM(near_list.shape, jnp.int32),
            pltpu.VMEM(coords.shape, f32),
            pltpu.VMEM(own.shape, bf16),
            pltpu.VMEM(own.shape, bf16),
            pltpu.VMEM(own.shape, bf16),
            pltpu.VMEM((vec_dev, points), f32),
            pltpu.SemaphoreType.DMA((5,)),
        ],
        compiler_params=params(60),
        cost_estimate=pl.CostEstimate(
            flops=2 * 512 * pairs, transcendentals=pairs, bytes_accessed=4 << 20
        ),
        name="near_field",
    )(first, near_list, coords, own, low, high)


def far_kernel(
    fine_list_hbm,
    coarse_list_hbm,
    got_hbm,
    fine_hbm,
    coarse_hbm,
    transfer_hbm,
    basis_hbm,
    near_hbm,
    out_ref,
    copies_ref,
    fine_list_ref,
    coarse_list_ref,
    got_ref,
    fine_ref,
    coarse_ref,
    transfer_ref,
    basis_ref,
    near_ref,
    sems,
    fine_sems,
    coarse_sems,
):
    leaf_dev, partners = fine_list_ref.shape
    width = 3
    rank, pts = basis_ref.shape[1:]
    half = got_ref.shape[1]
    copies = start_all(
        [
            (coarse_list_hbm, coarse_list_ref),
            (fine_list_hbm, fine_list_ref),
            (got_hbm, got_ref),
            (transfer_hbm, transfer_ref),
            (basis_hbm, basis_ref),
            (near_hbm, near_ref),
        ],
        sems,
    )

    def blocks(parent):
        two = pl.ds(2 * parent, 2)
        return (
            pltpu.make_async_copy(
                coarse_hbm.at[parent], coarse_ref.at[parent], coarse_sems.at[parent]
            ),
            pltpu.make_async_copy(fine_hbm.at[two], fine_ref.at[two], fine_sems.at[parent]),
        )

    for parent in range(leaf_dev // 2):
        for copy in blocks(parent):
            copy.start()
    wait_all(copies[:3])
    left = lax.broadcasted_iota(jnp.int32, (half, 2 * rank), 1) < rank

    def joined(first, second):
        first, second = first.astype(f32), second.astype(f32)
        return jnp.concatenate(
            [
                jnp.where(left, first, pltpu.roll(second, rank, 1)),
                jnp.where(left, pltpu.roll(first, rank, 1), second),
            ],
            axis=0,
        ).astype(bf16)

    def field(tiles_ref, list_ref, at, place):
        total = None
        for b in range(0, partners, 4):
            rows = [got_ref[place(list_ref[at, b + n])] for n in range(4)]
            rows = jnp.concatenate([joined(*rows[:2]), joined(*rows[2:])], axis=1)
            tiles = jnp.concatenate([tiles_ref[at, b + n] for n in range(4)], axis=1)
            part = lax.dot_general(rows, tiles, NT, preferred_element_type=f32)
            total = part if total is None else total + part
        return total

    parents = range(leaf_dev // 2)
    coarse, local = [], []
    for first in range(0, leaf_dev // 2, 2):
        group = range(first, first + 2)
        for parent in group:
            for copy in blocks(parent):
                copy.wait()
        for parent in group:
            coarse.append(
                field(coarse_ref, coarse_list_ref, parent, lambda r: r * width + 2).astype(bf16)
            )
        for leaf in range(2 * first, 2 * first + 2 * 2):
            local.append(field(fine_ref, fine_list_ref, leaf, lambda r: (r >> 1) * width + (r & 1)))
    wait_all(copies[3:])
    for leaf in range(leaf_dev):
        parent, child = leaf // 2, leaf % 2
        local[leaf] += lax.dot_general(
            coarse[parent], transfer_ref[parent, child], NT, preferred_element_type=f32
        )
    for leaf in range(leaf_dev):
        cols = slice(leaf * pts, (leaf + 1) * pts)
        far = jnp.dot(local[leaf].astype(bf16), basis_ref[leaf], preferred_element_type=f32)
        value = (near_ref[:, cols] + far).astype(bf16)
        out_ref[:, cols] = value
        for copy in range(copies_ref.shape[0]):
            copies_ref[copy, :, cols] = value


def far_field(
    far_fine, far_coarse, got, coupling_fine, coupling_coarse, transfer, basis, near, copies
):
    vec_dev, points = near.shape
    held = (got, coupling_fine, coupling_coarse, transfer, basis, near)
    parents = coupling_coarse.shape[0]
    return pl.pallas_call(
        far_kernel,
        out_shape=(
            jax.ShapeDtypeStruct((vec_dev, points), bf16),
            jax.ShapeDtypeStruct((copies, vec_dev, points), bf16),
        ),
        in_specs=[HB] * 8,
        out_specs=(VM, VM),
        scratch_shapes=[
            pltpu.SMEM(far_fine.shape, jnp.int32),
            pltpu.SMEM(far_coarse.shape, jnp.int32),
            *[pltpu.VMEM(a.shape, a.dtype) for a in held],
            pltpu.SemaphoreType.DMA((6,)),
            pltpu.SemaphoreType.DMA((parents,)),
            pltpu.SemaphoreType.DMA((parents,)),
        ],
        compiler_params=params(60),
        name="far_field",
    )(far_fine, far_coarse, *held)


def gram_kernel(me_ref, all_ref, out_ref):
    leaf_dev, vec_dev = out_ref.shape[:2]
    pts = all_ref.shape[1] // leaf_dev
    mine = pl.ds(pl.multiple_of(me_ref[0] * vec_dev, vec_dev), vec_dev)
    for leaf in range(leaf_dev):
        cols = slice(leaf * pts, (leaf + 1) * pts)
        out_ref[leaf] = lax.dot_general(
            all_ref[mine, cols], all_ref[:, cols], NT, preferred_element_type=f32
        ) * (1.0 / pts)


def gram(me, rows, vec_dev, leaf_dev):
    return pl.pallas_call(
        gram_kernel,
        out_shape=jax.ShapeDtypeStruct((leaf_dev, vec_dev, rows.shape[0]), f32),
        in_specs=[SM, VM],
        out_specs=VM,
        compiler_params=params(6),
        name="gram",
    )(me, rows)


def per_device(
    samples,
    coords,
    panel_area,
    quad_weight,
    leaf_basis,
    transfer,
    coupling_fine,
    coupling_coarse,
    near_list,
    send_fine,
    send_coarse,
    far_fine,
    far_coarse,
):
    vec_dev, points = samples.shape
    leaf_dev, rank, pts = leaf_basis.shape
    devices = lax.axis_size("leaf")
    groups = lax.axis_size("vec")
    device = lax.axis_index("leaf")

    own = source_rows(samples, coords, panel_area, quad_weight)
    forward = [(i, i + 1) for i in range(devices - 1)]
    backward = [(i + 1, i) for i in range(devices - 1)]
    low = lax.ppermute(own, "leaf", forward)
    high = lax.ppermute(own, "leaf", backward)

    sent = send_rows(send_fine, send_coarse, own, leaf_basis, transfer)
    half = sent.shape[1]
    sent, low, high = lax.optimization_barrier((sent, low, high))
    got = lax.all_to_all(
        sent.reshape(devices, -1, LANES), "leaf", split_axis=0, concat_axis=0, tiled=True
    ).reshape(-1, half, LANES)

    first = (device * leaf_dev - HW).astype(jnp.int32).reshape(1)
    near = near_field(first, near_list, coords, own, low, high, pts)
    sample_out, copies = far_field(
        far_fine, far_coarse, got, coupling_fine, coupling_coarse, transfer, leaf_basis, near, groups
    )
    rows = lax.all_to_all(copies, "vec", split_axis=0, concat_axis=0, tiled=True)
    me = lax.axis_index("vec").astype(jnp.int32).reshape(1)
    sample_gram = gram(me, rows.reshape(groups * vec_dev, points), vec_dev, leaf_dev)
    return (sample_out, sample_gram)


def solution(mesh):
    return jax.shard_map(
        per_device,
        mesh=mesh,
        in_specs=(
            P("vec", "leaf"),
            P(None, "leaf"),
            P("leaf"),
            P("leaf"),
            P("leaf", None, None),
            P("leaf", None, None, None),
            P("leaf", None, None, None),
            P("leaf", None, None, None),
            P("leaf", None),
            P("leaf", None),
            P("leaf", None),
            P("leaf", None),
            P("leaf", None),
        ),
        out_specs=(P("vec", "leaf"), P("leaf", "vec", None)),
        check_vma=False,
    )
```
